32 devices in a mesh: blk: 32 (over z, y, x, core), feat: 1.
Axes of the slice: x: 2, y: 2, z: 4, core: 2. Of those that a mesh axis runs over, the one named last changes fastest.
Arguments:
- activations: bfloat16 [5120, 4096], P('blk', 'feat'), may hold values from -6 to 6
- live_rows: int32 [32], replicated, may hold values from 1 to 160, as said below
- encoder_weight: bfloat16 [4096, 32768], P('feat', 'blk'), may hold values from -0.09375 to 0.09375
- encoder_bias: float32 [32768], P('blk'), may hold values from -3 to 3
- decoder_weight: bfloat16 [4, 1024, 32768], P(None, 'feat', 'blk'), may hold values from -0.09375 to 0.09375
- decoder_bias: float32 [32768], P('blk'), may hold values from -3 to 3
- targets: bfloat16 [640, 32768], P('feat', 'blk'), may hold values from -6 to 6
Outputs:
- reconstruction: float32 [640, 32768], P('feat', 'blk')
- decoder_grad: float32 [4, 1024, 32768], P(None, 'feat', 'blk')
The draws below stay inside these ranges and needn't reach their ends.
Inputs may be any that keep to these rules, and one draw needn't show every extreme that they name: `live_rows`: live rows of a block of 160 slots are its first ones; some block is full.
All inputs are finite; a program needn't handle non-finite values.
Results may differ from the reference program's by a relative error of at most 0.015.
Values may be sent and summed in bfloat16 or wider, within the bound.
A program may use at most 128 MiB of HBM per device.

```python
import jax
import jax.numpy as jnp
from jax import lax

D = 4096
F = 4096
G = 8
TOK_DEV = 160
OWN = 4
TOKG = 640
ROWS = 5120
N_BLK = 32
N_FEAT = 1


def draw_live_rows(key, part):
    blocks = ROWS // TOK_DEV
    counts = jax.random.randint(key, (blocks,), 1, TOK_DEV + 1)
    chosen = jax.random.randint(jax.random.fold_in(key, 7), (), 0, blocks)
    return counts.at[chosen].set(TOK_DEV).astype(jnp.int32)


def shard_levels(own_key, dims, split, smallest, top_value):
    def one(position, shards_of):
        steps = jax.random.uniform(jax.random.fold_in(jax.random.fold_in(own_key, 6), position), (shards_of,), jnp.float32, smallest / len(split), top_value / len(split))
        return jnp.repeat(jnp.exp(steps), dims[position] // shards_of).reshape((-1,) + (1,) * (len(dims) - position - 1))

    loudness = one(*split[0])
    for cut in split[1:]:
        loudness = loudness * one(*cut)
    return loudness


def gaussian(own_key, extent, scale, limit, shards=(), kind=jnp.bfloat16):
    entries = scale * jax.random.normal(own_key, extent, jnp.float32)
    if shards:
        entries = entries * shard_levels(own_key, extent, shards, -0.22, 0.18)
    return jnp.clip(entries, -limit, limit).astype(kind)


def setup_inputs(seed: int = 0) -> dict:
    keys = jax.random.split(jax.random.key(seed), 8)
    return {
        "activations": gaussian(keys[0], (ROWS, D), 1.0, 6.0, ((0, 32),)),
        "live_rows": draw_live_rows(jax.random.fold_in(keys[7], 71), 0),
        "encoder_weight": gaussian(keys[2], (D, G * F), D ** -0.5, 0.09375, ((1, 32),)),
        "encoder_bias": gaussian(keys[3], (G * F,), 0.5, 3.0, ((0, 32),), jnp.float32),
        "decoder_weight": gaussian(keys[4], (OWN, F // OWN, G * D), F ** -0.5, 0.09375, ((2, 32),)),
        "decoder_bias": gaussian(keys[5], (G * D,), 0.5, 3.0, ((0, 32),), jnp.float32),
        "targets": gaussian(keys[6], (TOKG, G * D), 1.0, 6.0, ((1, 32),)),
    }


def one_group(packed):
    inputs, live_mask, enc_block, enc_bias, dec_block, dec_bias, target_block = packed
    slab = D // N_FEAT
    row_count = inputs.shape[0]
    preact = jnp.zeros((row_count, F), jnp.float32)
    for share_index in range(N_FEAT):
        partial_value = jnp.dot(inputs[:, share_index * slab:(share_index + 1) * slab], enc_block[share_index * slab:(share_index + 1) * slab, :], preferred_element_type=jnp.float32)
        preact = preact + lax.optimization_barrier(partial_value.astype(jnp.bfloat16)).astype(jnp.float32)
    codes = (jax.nn.relu(preact + enc_bias[None, :]) * live_mask[:, None]).astype(jnp.bfloat16)
    owners = N_BLK // G
    per_share = F // owners // N_FEAT
    codes_split = codes.reshape(row_count, owners, N_FEAT, per_share)
    dec_split = dec_block.reshape(owners, N_FEAT, per_share, D)
    rebuilt = jnp.zeros((row_count, D), jnp.float32)
    for share_index in range(N_FEAT):
        left = codes_split[:, :, share_index, :].reshape(row_count, owners * per_share)
        right = dec_split[:, share_index].reshape(owners * per_share, D)
        partial_value = jnp.dot(left, right, preferred_element_type=jnp.float32)
        rebuilt = rebuilt + lax.optimization_barrier(partial_value.astype(jnp.bfloat16)).astype(jnp.float32)
    rebuilt = rebuilt + dec_bias[None, :]
    residual = ((rebuilt - target_block.astype(jnp.float32)) * live_mask[:, None]).astype(jnp.bfloat16)
    gradient = jnp.dot(codes.T, residual, preferred_element_type=jnp.float32)
    return rebuilt, gradient


def reference(activations, live_rows, encoder_weight, encoder_bias, decoder_weight, decoder_bias, targets):
    owners = N_BLK // G
    positions = jnp.arange(TOK_DEV, dtype=jnp.int32)
    live_mask = (positions[None, :] < live_rows[:, None]).astype(jnp.float32).reshape(G, TOKG)
    inputs = activations.reshape(G, TOKG, D)
    enc_blocks = encoder_weight.reshape(D, G, F).transpose(1, 0, 2)
    enc_biases = encoder_bias.reshape(G, F)
    dec_blocks = decoder_weight.reshape(owners, F // owners, G, D).transpose(2, 0, 1, 3).reshape(G, F, D)
    dec_biases = decoder_bias.reshape(G, D)
    target_blocks = targets.reshape(TOKG, G, D).transpose(1, 0, 2)
    rebuilt, gradient = lax.map(one_group, (inputs, live_mask, enc_blocks, enc_biases, dec_blocks, dec_biases, target_blocks))
    reconstruction = rebuilt.transpose(1, 0, 2).reshape(TOKG, G * D)
    decoder_grad = gradient.reshape(G, owners, F // owners, D).transpose(1, 2, 0, 3).reshape(owners, F // owners, G * D)
    return reconstruction, decoder_grad
```

```python
import functools

import jax
import jax.numpy as jnp
from jax import lax
from jax.experimental import pallas as pl
from jax.experimental.pallas import tpu as pltpu
from jax.sharding import PartitionSpec as P

G = 8
MESH = pl.DeviceIdType.MESH


def gather_kernel(
    pieces,
    act_hbm,
    live_ref,
    enc_hbm,
    bias_ref,
    dec_hbm,
    codes_hbm,
    summed_hbm,
    acts,
    enc,
    dec,
    codes,
    part,
    summed,
    load_sem,
    s1_send,
    s1_recv,
    s2_send,
    s2_recv,
    s3_send,
    s3_recv,
    t1_send,
    t1_recv,
    t2_send,
    t2_recv,
    t3_send,
    t3_recv,
    out_sem,
):
    position = lax.axis_index("blk")
    share = lax.axis_index("feat")
    base = position // 4 * 4
    me = position % 4
    core = me % 2
    home = me - core
    away = 2 - home
    twin = home + 1 - core
    peer = away + core
    peer_twin = away + 1 - core
    on_chip = (base + twin, share)
    across = (base + peer, share)

    rows = acts.shape[1]
    piece = rows // pieces
    width = enc.shape[1]
    tile = min(256, width)
    tiles = width // tile

    def at_piece(h):
        return pl.ds(h * piece, piece)

    load_act = pltpu.make_async_copy(act_hbm, acts.at[me], load_sem.at[0])
    load_enc = pltpu.make_async_copy(enc_hbm, enc, load_sem.at[1])
    load_dec = pltpu.make_async_copy(dec_hbm, dec, load_sem.at[2])
    load_act.start()
    load_enc.start()
    load_dec.start()

    barrier = pltpu.get_barrier_semaphore()
    for neighbour in (on_chip, across):
        pl.semaphore_signal(barrier, inc=1, device_id=neighbour, device_id_type=MESH)
    pl.semaphore_wait(barrier, 2)

    def remote(src, dst, send, recv, to):
        return pltpu.make_async_remote_copy(
            src_ref=src,
            dst_ref=dst,
            send_sem=send,
            recv_sem=recv,
            device_id=to,
            device_id_type=MESH,
        )

    def s1(b):
        return remote(act_hbm, acts.at[b], s1_send.at[0], s1_recv.at[0], on_chip)

    def s2(b, h):
        return remote(
            act_hbm.at[at_piece(h)],
            acts.at[b, at_piece(h)],
            s2_send.at[h],
            s2_recv.at[h],
            across,
        )

    def s3(b, h):
        ref = acts.at[b, at_piece(h)]
        return remote(ref, ref, s3_send.at[h], s3_recv.at[h], on_chip)

    def t1(f, b):
        ref = codes.at[f, b]
        return remote(ref, ref, t1_send.at[b], t1_recv.at[b], on_chip)

    def t2(f, b, h):
        ref = codes.at[f, b, at_piece(h)]
        return remote(ref, ref, t2_send.at[b, h], t2_recv.at[b, h], across)

    def t3(f, b, h):
        ref = codes.at[f, b, at_piece(h)]
        return remote(ref, ref, t3_send.at[b, h], t3_recv.at[b, h], on_chip)

    for h in range(pieces):
        s2(me, h).start()
    s1(me).start()

    def encode(b):
        live = live_ref[base + b]
        keep = lax.broadcasted_iota(jnp.int32, (rows, tile), 0) < live

        def column(n, carry):
            at = pl.ds(pl.multiple_of(n * tile, tile), tile)
            product = jnp.dot(acts[b], enc[:, at], preferred_element_type=jnp.float32)
            value = product.astype(jnp.bfloat16).astype(jnp.float32) + bias_ref[:, at]
            value = jnp.where(keep, jnp.maximum(value, 0.0), 0.0)
            codes[me, b, :, at] = value.astype(jnp.bfloat16)
            return carry

        lax.fori_loop(0, tiles, column, 0)

    def product_of(fs, b, at, h=None):
        total = None
        for f in fs:
            left = codes[f, b] if h is None else codes[f, b, at_piece(h)]
            term = jnp.dot(left, dec[f, :, at], preferred_element_type=jnp.float32)
            total = term if total is None else total + term
        return total

    def out_codes(b, h):
        return pltpu.make_async_copy(
            codes.at[:, b, at_piece(h)], codes_hbm.at[:, b, at_piece(h)], out_sem.at[0, b, h]
        )

    def out_summed(b, h):
        return pltpu.make_async_copy(
            summed.at[b, at_piece(h)], summed_hbm.at[b, at_piece(h)], out_sem.at[1, b, h]
        )

    load_act.wait()
    load_enc.wait()
    encode(me)
    s1(twin).wait_recv()
    t1(me, me).start()
    encode(twin)
    t1(me, twin).start()
    for b in (home, home + 1):
        for h in range(pieces):
            t2(me, b, h).start()
    t1(twin, home).wait_recv()
    t1(twin, home + 1).wait_recv()
    load_dec.wait()

    def half(b, slot):
        def column(n, carry):
            at = pl.ds(pl.multiple_of(n * tile, tile), tile)
            part[slot, :, at] = product_of((home, home + 1), b, at)
            return carry

        lax.fori_loop(0, tiles, column, 0)

    def half_step(slot, carry):
        half(home + slot, slot)
        return carry

    lax.fori_loop(0, 2, half_step, 0)

    for h in range(pieces):
        s2(peer, h).wait_recv()
        s3(peer, h).start()
    encode(peer)
    t1(me, peer).start()
    for h in range(pieces):
        s3(peer_twin, h).wait_recv()
    encode(peer_twin)
    t1(me, peer_twin).start()
    for b in (away, away + 1):
        for h in range(pieces):
            t2(me, b, h).start()
    for b in (away, away + 1):
        for h in range(pieces):
            t2(peer, b, h).wait_recv()
            t3(peer, b, h).start()
    t1(twin, away).wait_recv()
    t1(twin, away + 1).wait_recv()

    def away_step(i, carry):
        b = away + i
        for h in range(pieces):
            t3(peer_twin, b, h).wait_recv()
            out_codes(b, h).start()

        def column(n, inner):
            at = pl.ds(pl.multiple_of(n * tile, tile), tile)
            summed[b, :, at] = product_of((0, 1, 2, 3), b, at).astype(jnp.bfloat16)
            return inner

        lax.fori_loop(0, tiles, column, 0)
        for h in range(pieces):
            out_summed(b, h).start()
        return carry

    lax.fori_loop(0, 2, away_step, 0)

    def home_step(i, carry):
        b = home + i
        for h in range(pieces):
            t2(peer, b, h).wait_recv()
            t3(peer, b, h).start()
            t3(peer_twin, b, h).wait_recv()
            out_codes(b, h).start()

            def column(n, inner):
                at = pl.ds(pl.multiple_of(n * tile, tile), tile)
                total = part[i, at_piece(h), at] + product_of((away, away + 1), b, at, h)
                summed[b, at_piece(h), at] = total.astype(jnp.bfloat16)
                return inner

            lax.fori_loop(0, tiles, column, 0)
            out_summed(b, h).start()
        return carry

    lax.fori_loop(0, 2, home_step, 0)

    s1(me).wait_send()
    for h in range(pieces):
        s2(me, h).wait_send()
        s3(peer, h).wait_send()
    for b in range(4):
        t1(me, b).wait_send()
        for h in range(pieces):
            t2(me, b, h).wait_send()
            t3(peer, b, h).wait_send()
            out_codes(b, h).wait()
            out_summed(b, h).wait()


def gradient_kernel(
    live_ref, codes_ref, summed_ref, bias_ref, targets_ref, grad_ref, rebuilt_hbm, residual, rebuilt, sem
):
    step = pl.program_id(0)
    copy = pltpu.make_async_copy(rebuilt, rebuilt_hbm, sem)

    @pl.when(step == 0)
    def _():
        base = lax.axis_index("blk") // 4 * 4
        rows, width = summed_ref.shape[1:]
        for b in range(4):
            at = pl.ds(b * rows, rows)
            whole = summed_ref[b].astype(jnp.float32) + bias_ref[...]
            rebuilt[at, :] = whole
            keep = lax.broadcasted_iota(jnp.int32, (rows, width), 0) < live_ref[base + b]
            error = jnp.where(keep, whole - targets_ref[at, :].astype(jnp.float32), 0.0)
            residual[at, :] = error.astype(jnp.bfloat16)
        copy.start()

    grad_ref[0] = lax.dot_general(
        codes_ref[0], residual[...], (((0,), (0,)), ((), ())), preferred_element_type=jnp.float32
    )

    @pl.when(step == pl.num_programs(0) - 1)
    def _():
        copy.wait()


def four_owners(
    activations, live_rows, encoder_weight, encoder_bias, decoder_weight, decoder_bias, targets
):
    rows, depth = activations.shape
    features = encoder_weight.shape[1]
    width = decoder_weight.shape[2]
    tokens = targets.shape[0]
    pieces = 2 if rows % 32 == 0 else 1
    any_space = pl.BlockSpec(memory_space=pl.ANY)
    in_vmem = pl.BlockSpec(memory_space=pltpu.VMEM)
    in_smem = pl.BlockSpec(memory_space=pltpu.SMEM)
    dma = pltpu.SemaphoreType.DMA
    bf16 = jnp.bfloat16
    codes, summed = pl.pallas_call(
        functools.partial(gather_kernel, pieces),
        out_shape=(
            jax.ShapeDtypeStruct((4, 4, rows, features), bf16),
            jax.ShapeDtypeStruct((4, rows, width), bf16),
        ),
        in_specs=[any_space, in_smem, any_space, in_vmem, any_space],
        out_specs=(any_space, any_space),
        scratch_shapes=[
            pltpu.VMEM((4, rows, depth), bf16),
            pltpu.VMEM((depth, features), bf16),
            pltpu.VMEM((4, features, width), bf16),
            pltpu.VMEM((4, 4, rows, features), bf16),
            pltpu.VMEM((2, rows, width), jnp.float32),
            pltpu.VMEM((4, rows, width), bf16),
            dma((3,)),
            dma((1,)),
            dma((1,)),
            dma((pieces,)),
            dma((pieces,)),
            dma((pieces,)),
            dma((pieces,)),
            dma((4,)),
            dma((4,)),
            dma((4, pieces)),
            dma((4, pieces)),
            dma((4, pieces)),
            dma((4, pieces)),
            dma((2, 4, pieces)),
        ],
        compiler_params=pltpu.CompilerParams(
            collective_id=0, has_side_effects=True, vmem_limit_bytes=60 * 1024 * 1024
        ),
        name="gather_codes",
    )(activations, live_rows, encoder_weight, encoder_bias[None, :], decoder_weight)

    span = min(512, features)
    per = features // span
    grad, rebuilt = pl.pallas_call(
        gradient_kernel,
        grid=(4 * per,),
        out_shape=(
            jax.ShapeDtypeStruct((4, features, width), jnp.float32),
            jax.ShapeDtypeStruct((tokens, width), jnp.float32),
        ),
        in_specs=[
            in_smem,
            pl.BlockSpec((1, tokens, span), lambda i: (i // per, 0, i % per)),
            in_vmem,
            in_vmem,
            in_vmem,
        ],
        out_specs=(pl.BlockSpec((1, span, width), lambda i: (i // per, i % per, 0)), any_space),
        scratch_shapes=[
            pltpu.VMEM((tokens, width), bf16),
            pltpu.VMEM((tokens, width), jnp.float32),
            dma(()),
        ],
        compiler_params=pltpu.CompilerParams(
            dimension_semantics=("arbitrary",), vmem_limit_bytes=60 * 1024 * 1024
        ),
        name="gradient",
    )(live_rows, codes.reshape(4, tokens, features), summed, decoder_bias[None, :], targets)
    return rebuilt, grad


def from_partner(shard, axis, distance):
    return lax.ppermute(shard, axis, [(i, i ^ 1 << distance) for i in range(lax.axis_size(axis))])


def group_rows(block, levels, position):
    for bit in range(levels):
        other = from_partner(block, "blk", bit)
        upper = position >> bit & 1 == 1
        block = jnp.where(
            upper, jnp.concatenate([other, block], 0), jnp.concatenate([block, other], 0)
        )
    return block


def general(
    activations, live_rows, encoder_weight, encoder_bias, decoder_weight, decoder_bias, targets
):
    owners = lax.axis_size("blk") // G
    levels = owners.bit_length() - 1
    shares = lax.axis_size("feat")
    position = lax.axis_index("blk")
    share_index = lax.axis_index("feat")
    group_index = position // owners
    tok_rows = activations.shape[0]
    counts = lax.dynamic_slice_in_dim(live_rows, group_index * owners, owners)
    positions = jnp.arange(tok_rows, dtype=jnp.int32)
    live_mask = (positions[None, :] < counts[:, None]).astype(jnp.float32).reshape(-1)
    gathered = group_rows(activations, levels, position)
    per_share = encoder_weight.shape[1] // shares
    bias_share = lax.dynamic_slice_in_dim(encoder_bias, share_index * per_share, per_share)
    columns = encoder_weight
    whole = lax.psum(
        lax.dot_general(
            columns, gathered, (((0,), (1,)), ((), ())), preferred_element_type=jnp.float32
        ).astype(jnp.bfloat16),
        "feat",
    ).astype(jnp.float32)
    preact = lax.dynamic_slice_in_dim(whole, share_index * per_share, per_share, 0)
    codes_by_feature = (jax.nn.relu(preact + bias_share[:, None]) * live_mask[None, :]).astype(
        jnp.bfloat16
    )
    codes_all = group_rows(codes_by_feature, levels, position)
    decoder_rows = decoder_weight.reshape(-1, decoder_weight.shape[2])
    block_rows = gathered.shape[0] // shares
    columns = codes_all
    summed = lax.psum_scatter(
        lax.dot_general(
            columns, decoder_rows, (((0,), (0,)), ((), ())), preferred_element_type=jnp.float32
        ).astype(jnp.bfloat16),
        "feat",
        scatter_dimension=0,
        tiled=True,
    ).astype(jnp.float32)
    rebuilt = summed + decoder_bias[None, :]
    mask_block = lax.dynamic_slice_in_dim(live_mask, share_index * block_rows, block_rows)
    residual = ((rebuilt - targets.astype(jnp.float32)) * mask_block[:, None]).astype(jnp.bfloat16)
    columns = codes_all
    gradient = jnp.dot(
        columns,
        lax.all_gather(residual, "feat", axis=0, tiled=True),
        preferred_element_type=jnp.float32,
    )
    return (rebuilt, gradient.reshape(decoder_weight.shape))


def solution(mesh):
    in_specs = (
        P("blk", "feat"),
        P(),
        P("feat", "blk"),
        P("blk"),
        P(None, "feat", "blk"),
        P("blk"),
        P("feat", "blk"),
    )
    out_specs = (P("feat", "blk"), P(None, "feat", "blk"))
    fused = mesh.shape["blk"] // G == 4 and mesh.shape["feat"] == 1
    return jax.shard_map(
        four_owners if fused else general,
        mesh=mesh,
        in_specs=in_specs,
        out_specs=out_specs,
        check_vma=False,
    )
```

```python
import functools

import jax
import jax.numpy as jnp
from jax import lax
from jax.experimental import pallas as pl
from jax.experimental.pallas import tpu as pltpu
from jax.sharding import PartitionSpec as P

G = 8
MESH = pl.DeviceIdType.MESH


def gather_kernel(
    pieces,
    act_hbm,
    live_ref,
    enc_hbm,
    bias_ref,
    dec_hbm,
    dec_bias_ref,
    targets_hbm,
    codes_out,
    summed,
    grad,
    acts,
    enc,
    dec,
    codes,
    part,
    targets,
    residual,
    load_sem,
    s1_send,
    s1_recv,
    s2_send,
    s2_recv,
    s3_send,
    s3_recv,
    t1_send,
    t1_recv,
    t2_send,
    t2_recv,
    t3_send,
    t3_recv,
    out_sem,
):
    position = lax.axis_index("blk")
    share = lax.axis_index("feat")
    base = position // 4 * 4
    me = position % 4
    core = me % 2
    home = me - core
    away = 2 - home
    twin = home + 1 - core
    peer = away + core
    peer_twin = away + 1 - core
    rows = acts.shape[1]
    on_chip = (base + twin, share)
    across = (base + peer, share)

    piece = rows // pieces
    width = enc.shape[1]
    tile = min(256, width)
    tiles = width // tile

    def at_piece(h):
        return pl.ds(h * piece, piece)

    load_act = pltpu.make_async_copy(act_hbm, acts.at[me], load_sem.at[0])
    load_enc = pltpu.make_async_copy(enc_hbm, enc, load_sem.at[1])
    load_dec = pltpu.make_async_copy(dec_hbm, dec, load_sem.at[2])
    load_targets = pltpu.make_async_copy(
        targets_hbm.at[pl.ds(pl.multiple_of(away * rows, 16), 2 * rows)], targets, load_sem.at[3]
    )
    load_act.start()
    load_enc.start()
    load_dec.start()
    load_targets.start()

    barrier = pltpu.get_barrier_semaphore()
    for neighbour in (on_chip, across):
        pl.semaphore_signal(barrier, inc=1, device_id=neighbour, device_id_type=MESH)
    pl.semaphore_wait(barrier, 2)

    def remote(src, dst, send, recv, to):
        return pltpu.make_async_remote_copy(
            src_ref=src,
            dst_ref=dst,
            send_sem=send,
            recv_sem=recv,
            device_id=to,
            device_id_type=MESH,
        )

    def s1(b):
        return remote(act_hbm, acts.at[b], s1_send.at[0], s1_recv.at[0], on_chip)

    def s2(b, h):
        return remote(
            act_hbm.at[at_piece(h)],
            acts.at[b, at_piece(h)],
            s2_send.at[h],
            s2_recv.at[h],
            across,
        )

    def s3(b, h):
        ref = acts.at[b, at_piece(h)]
        return remote(ref, ref, s3_send.at[h], s3_recv.at[h], on_chip)

    def t1(f, b):
        ref = codes.at[f, b]
        return remote(ref, ref, t1_send.at[b], t1_recv.at[b], on_chip)

    def t2(f, b, h):
        ref = codes.at[f, b, at_piece(h)]
        return remote(ref, ref, t2_send.at[b, h], t2_recv.at[b, h], across)

    def t3(f, b, h):
        ref = codes.at[f, b, at_piece(h)]
        return remote(ref, ref, t3_send.at[b, h], t3_recv.at[b, h], on_chip)

    for h in range(pieces):
        s2(me, h).start()
    s1(me).start()

    def encode(b):
        live = live_ref[base + b]
        keep = lax.broadcasted_iota(jnp.int32, (rows, tile), 0) < live

        def column(n, carry):
            at = pl.ds(pl.multiple_of(n * tile, tile), tile)
            product = jnp.dot(acts[b], enc[:, at], preferred_element_type=jnp.float32)
            value = product.astype(jnp.bfloat16).astype(jnp.float32) + bias_ref[:, at]
            value = jnp.where(keep, jnp.maximum(value, 0.0), 0.0)
            codes[me, b, :, at] = value.astype(jnp.bfloat16)
            return carry

        lax.fori_loop(0, tiles, column, 0)

    def product_of(fs, b, at, h=None):
        total = None
        for f in fs:
            left = codes[f, b] if h is None else codes[f, b, at_piece(h)]
            term = jnp.dot(left, dec[f, :, at], preferred_element_type=jnp.float32)
            total = term if total is None else total + term
        return total

    def out_codes(i, h):
        return pltpu.make_async_copy(
            codes.at[:, home + i, at_piece(h)], codes_out.at[:, i, at_piece(h)], out_sem.at[i, h]
        )

    load_act.wait()
    load_enc.wait()
    encode(me)
    s1(twin).wait_recv()
    t1(me, me).start()
    encode(twin)
    t1(me, twin).start()
    for b in (home, home + 1):
        for h in range(pieces):
            t2(me, b, h).start()
    t1(twin, home).wait_recv()
    t1(twin, home + 1).wait_recv()
    load_dec.wait()

    def half(b, slot):
        def column(n, carry):
            at = pl.ds(pl.multiple_of(n * tile, tile), tile)
            part[slot, :, at] = product_of((home, home + 1), b, at)
            return carry

        lax.fori_loop(0, tiles, column, 0)

    def half_step(slot, carry):
        half(home + slot, slot)
        return carry

    lax.fori_loop(0, 2, half_step, 0)

    for h in range(pieces):
        s2(peer, h).wait_recv()
        s3(peer, h).start()
    encode(peer)
    t1(me, peer).start()
    for h in range(pieces):
        s3(peer_twin, h).wait_recv()
    encode(peer_twin)
    t1(me, peer_twin).start()
    for b in (away, away + 1):
        for h in range(pieces):
            t2(me, b, h).start()
    for b in (away, away + 1):
        for h in range(pieces):
            t2(peer, b, h).wait_recv()
            t3(peer, b, h).start()
    t1(twin, away).wait_recv()
    t1(twin, away + 1).wait_recv()

    def away_step(i, carry):
        b = away + i
        for h in range(pieces):
            t3(peer_twin, b, h).wait_recv()
        keep = lax.broadcasted_iota(jnp.int32, (rows, tile), 0) < live_ref[base + b]
        here = pl.ds(pl.multiple_of(i * rows, 16), rows)

        def column(n, inner):
            at = pl.ds(pl.multiple_of(n * tile, tile), tile)
            rounded = product_of((0, 1, 2, 3), b, at).astype(jnp.bfloat16)
            summed[b, :, at] = rounded
            whole = rounded.astype(jnp.float32) + dec_bias_ref[:, at]
            error = jnp.where(keep, whole - targets[here, at].astype(jnp.float32), 0.0)
            residual[here, at] = error.astype(jnp.bfloat16)
            return inner

        lax.fori_loop(0, tiles, column, 0)
        return carry

    load_targets.wait()
    lax.fori_loop(0, 2, away_step, 0)

    def gradient_step(k, carry):
        f = k // tiles
        at = pl.ds(pl.multiple_of(k % tiles * tile, tile), tile)
        left = codes[f, pl.ds(away, 2), :, at].reshape(2 * rows, tile)
        grad[f, at, :] = lax.dot_general(
            left, residual[...], (((0,), (0,)), ((), ())), preferred_element_type=jnp.float32
        )
        return carry

    lax.fori_loop(0, 4 * tiles, gradient_step, 0)

    def home_step(i, carry):
        b = home + i
        for h in range(pieces):
            t2(peer, b, h).wait_recv()
            t3(peer, b, h).start()
            t3(peer_twin, b, h).wait_recv()
            out_codes(i, h).start()

            def column(n, inner):
                at = pl.ds(pl.multiple_of(n * tile, tile), tile)
                total = part[i, at_piece(h), at] + product_of((away, away + 1), b, at, h)
                summed[b, at_piece(h), at] = total.astype(jnp.bfloat16)
                return inner

            lax.fori_loop(0, tiles, column, 0)
        return carry

    lax.fori_loop(0, 2, home_step, 0)

    s1(me).wait_send()
    for h in range(pieces):
        s2(me, h).wait_send()
        s3(peer, h).wait_send()
    for b in range(4):
        t1(me, b).wait_send()
        for h in range(pieces):
            t2(me, b, h).wait_send()
            t3(peer, b, h).wait_send()
    for i in range(2):
        for h in range(pieces):
            out_codes(i, h).wait()


def gradient_kernel(
    live_ref,
    codes_ref,
    summed_ref,
    bias_ref,
    targets_ref,
    part_ref,
    grad_ref,
    rebuilt_hbm,
    residual,
    rebuilt,
    sem,
):
    step = pl.program_id(0)
    copy = pltpu.make_async_copy(rebuilt, rebuilt_hbm, sem)
    span = grad_ref.shape[1]
    per = part_ref.shape[1] // span

    @pl.when(step == 0)
    def _():
        position = lax.axis_index("blk")
        base = position // 4 * 4
        home = position % 4 // 2 * 2
        rows, width = summed_ref.shape[1:]
        for i in range(2):
            b = home + i
            whole = summed_ref[b].astype(jnp.float32) + bias_ref[...]
            keep = lax.broadcasted_iota(jnp.int32, (rows, width), 0) < live_ref[base + b]
            wanted = targets_ref[pl.ds(pl.multiple_of(b * rows, 16), rows), :]
            error = jnp.where(keep, whole - wanted.astype(jnp.float32), 0.0)
            residual[pl.ds(i * rows, rows), :] = error.astype(jnp.bfloat16)
        for b in range(4):
            rebuilt[pl.ds(b * rows, rows), :] = summed_ref[b].astype(jnp.float32) + bias_ref[...]
        copy.start()

    at = pl.ds(pl.multiple_of(step % per * span, span), span)
    grad_ref[0] = part_ref[step // per, at, :] + lax.dot_general(
        codes_ref[step // per, :, at], residual[...], (((0,), (0,)), ((), ())), preferred_element_type=jnp.float32
    )

    @pl.when(step == pl.num_programs(0) - 1)
    def _():
        copy.wait()


def four_owners(
    activations, live_rows, encoder_weight, encoder_bias, decoder_weight, decoder_bias, targets
):
    rows, depth = activations.shape
    features = encoder_weight.shape[1]
    width = decoder_weight.shape[2]
    tokens = targets.shape[0]
    pieces = 2 if rows % 32 == 0 else 1
    any_space = pl.BlockSpec(memory_space=pl.ANY)
    in_vmem = pl.BlockSpec(memory_space=pltpu.VMEM)
    in_smem = pl.BlockSpec(memory_space=pltpu.SMEM)
    dma = pltpu.SemaphoreType.DMA
    bf16 = jnp.bfloat16
    codes, summed, part = pl.pallas_call(
        functools.partial(gather_kernel, pieces),
        out_shape=(
            pltpu.VMEM((4, 2, rows, features), bf16),
            pltpu.VMEM((4, rows, width), bf16),
            pltpu.VMEM((4, features, width), jnp.float32),
        ),
        in_specs=[any_space, in_smem, any_space, in_vmem, any_space, in_vmem, any_space],
        out_specs=(in_vmem, in_vmem, in_vmem),
        scratch_shapes=[
            pltpu.VMEM((4, rows, depth), bf16),
            pltpu.VMEM((depth, features), bf16),
            pltpu.VMEM((4, features, width), bf16),
            pltpu.VMEM((4, 4, rows, features), bf16),
            pltpu.VMEM((2, rows, width), jnp.float32),
            pltpu.VMEM((2 * rows, width), bf16),
            pltpu.VMEM((2 * rows, width), bf16),
            dma((4,)),
            dma((1,)),
            dma((1,)),
            dma((pieces,)),
            dma((pieces,)),
            dma((pieces,)),
            dma((pieces,)),
            dma((4,)),
            dma((4,)),
            dma((4, pieces)),
            dma((4, pieces)),
            dma((4, pieces)),
            dma((4, pieces)),
            dma((2, pieces)),
        ],
        compiler_params=pltpu.CompilerParams(
            collective_id=0, has_side_effects=True, vmem_limit_bytes=38 * 1024 * 1024
        ),
        name="gather_codes",
    )(activations, live_rows, encoder_weight, encoder_bias[None, :], decoder_weight, decoder_bias[None, :], targets)

    span = min(512, features)
    per = features // span
    grad, rebuilt = pl.pallas_call(
        gradient_kernel,
        grid=(4 * per,),
        out_shape=(
            jax.ShapeDtypeStruct((4, features, width), jnp.float32),
            jax.ShapeDtypeStruct((tokens, width), jnp.float32),
        ),
        in_specs=[
            in_smem,
            in_vmem,
            in_vmem,
            in_vmem,
            in_vmem,
            in_vmem,
        ],
        out_specs=(pl.BlockSpec((1, span, width), lambda i: (i // per, i % per, 0)), any_space),
        scratch_shapes=[
            pltpu.VMEM((2 * rows, width), bf16),
            pltpu.VMEM((tokens, width), jnp.float32),
            dma(()),
        ],
        compiler_params=pltpu.CompilerParams(
            dimension_semantics=("arbitrary",), vmem_limit_bytes=24 * 1024 * 1024
        ),
        name="gradient",
    )(live_rows, codes.reshape(4, 2 * rows, features), summed, decoder_bias[None, :], targets, part)
    return rebuilt, grad


def from_partner(shard, axis, distance):
    return lax.ppermute(shard, axis, [(i, i ^ 1 << distance) for i in range(lax.axis_size(axis))])


def group_rows(block, levels, position):
    for bit in range(levels):
        other = from_partner(block, "blk", bit)
        upper = position >> bit & 1 == 1
        block = jnp.where(
            upper, jnp.concatenate([other, block], 0), jnp.concatenate([block, other], 0)
        )
    return block


def general(
    activations, live_rows, encoder_weight, encoder_bias, decoder_weight, decoder_bias, targets
):
    owners = lax.axis_size("blk") // G
    levels = owners.bit_length() - 1
    shares = lax.axis_size("feat")
    position = lax.axis_index("blk")
    share_index = lax.axis_index("feat")
    group_index = position // owners
    tok_rows = activations.shape[0]
    counts = lax.dynamic_slice_in_dim(live_rows, group_index * owners, owners)
    positions = jnp.arange(tok_rows, dtype=jnp.int32)
    live_mask = (positions[None, :] < counts[:, None]).astype(jnp.float32).reshape(-1)
    gathered = group_rows(activations, levels, position)
    per_share = encoder_weight.shape[1] // shares
    bias_share = lax.dynamic_slice_in_dim(encoder_bias, share_index * per_share, per_share)
    columns = encoder_weight
    whole = lax.psum(
        lax.dot_general(
            columns, gathered, (((0,), (1,)), ((), ())), preferred_element_type=jnp.float32
        ).astype(jnp.bfloat16),
        "feat",
    ).astype(jnp.float32)
    preact = lax.dynamic_slice_in_dim(whole, share_index * per_share, per_share, 0)
    codes_by_feature = (jax.nn.relu(preact + bias_share[:, None]) * live_mask[None, :]).astype(
        jnp.bfloat16
    )
    codes_all = group_rows(codes_by_feature, levels, position)
    decoder_rows = decoder_weight.reshape(-1, decoder_weight.shape[2])
    block_rows = gathered.shape[0] // shares
    columns = codes_all
    summed = lax.psum_scatter(
        lax.dot_general(
            columns, decoder_rows, (((0,), (0,)), ((), ())), preferred_element_type=jnp.float32
        ).astype(jnp.bfloat16),
        "feat",
        scatter_dimension=0,
        tiled=True,
    ).astype(jnp.float32)
    rebuilt = summed + decoder_bias[None, :]
    mask_block = lax.dynamic_slice_in_dim(live_mask, share_index * block_rows, block_rows)
    residual = ((rebuilt - targets.astype(jnp.float32)) * mask_block[:, None]).astype(jnp.bfloat16)
    columns = codes_all
    gradient = jnp.dot(
        columns,
        lax.all_gather(residual, "feat", axis=0, tiled=True),
        preferred_element_type=jnp.float32,
    )
    return (rebuilt, gradient.reshape(decoder_weight.shape))


def solution(mesh):
    in_specs = (
        P("blk", "feat"),
        P(),
        P("feat", "blk"),
        P("blk"),
        P(None, "feat", "blk"),
        P("blk"),
        P("feat", "blk"),
    )
    out_specs = (P("feat", "blk"), P(None, "feat", "blk"))
    fused = mesh.shape["blk"] // G == 4 and mesh.shape["feat"] == 1
    return jax.shard_map(
        four_owners if fused else general,
        mesh=mesh,
        in_specs=in_specs,
        out_specs=out_specs,
        check_vma=False,
    )
```
